32 devices in a mesh: rep: 2 (over x), walk: 16 (over z, y, core).
Axes of the slice: x: 2, y: 2, z: 4, core: 2. Of those that a mesh axis runs over, the one named last changes fastest.
Arguments:
- greens: bfloat16 [32, 64, 384], P(('rep', 'walk')), parts along dimension 0, may hold values from -6 to 6
- source: int32 [64], P(('rep', 'walk')), parts along dimension 0, may hold values from 0 to 15, as said below
- counts: int32 [32], P('rep'), parts along dimension 0, may hold values from 1 to 2, as said below
- cholesky: bfloat16 [512, 64, 384], P('walk'), may hold values from -0.0390625 to 0.0390625
Outputs:
- relocated: bfloat16 [64, 64, 384], P(('rep', 'walk')), parts along dimension 0
- exchange_energy: float32 [64], P(('rep', 'walk')), parts along dimension 0
- force_bias: float32 [64, 512], P(('rep', 'walk')), parts along dimension 0
The draws below stay inside these ranges and needn't reach their ends.
There are 2 independent parts, one for each index of `rep`. The reference program is written for one: setup_inputs(seed, part) draws one part's arguments, and reference() takes and returns one part's arrays. A program takes and returns all parts, laid end to end along the dimension named above; an argument that names none is the same for every part. Nothing has to cross between parts.
Inputs may be any that keep to these rules, and one draw needn't show every extreme that they name: `source`: slot s belongs to walk device s div 2. Its walker comes from that device or one of the two devices beside it along the closed loop of walk devices. Slots beyond a device's count also name some walker. Slots 0 to counts[d] - 1 of device d are live.
All inputs are finite; a program needn't handle non-finite values.
Results may differ from the reference program's by a relative error of at most 0.001.
Values may be sent and summed in bfloat16 or wider, within the bound.
A program may use at most 64 MiB of HBM per device.

```python
import jax
import jax.numpy as jnp
from jax import lax

NOCC = 64
NORB = 384
WSLOT = 1
CAP = 2
NW = 16
NW2 = 32
NCHOL = 512
N_WALK = 16


def population(key):
    base_key = jax.random.fold_in(key, 11)
    k_count, k_full, k_offset, k_local = jax.random.split(base_key, 4)
    counts = jax.random.randint(k_count, (N_WALK,), WSLOT, 2 * WSLOT + 1)
    fullest = jax.random.randint(k_full, (), 0, N_WALK)
    counts = counts.at[fullest].set(2 * WSLOT)
    counts = counts.at[(fullest + 1) % N_WALK].set(WSLOT)
    owner = jnp.arange(NW2) // CAP
    offset = jax.random.randint(k_offset, (NW2,), -1, 2)
    offset = offset.at[0].set(-1)
    offset = offset.at[CAP].set(-1)
    src_dev = (owner + offset) % N_WALK
    local_idx = jax.random.randint(k_local, (NW2,), 0, WSLOT)
    local_idx = local_idx.at[0].set(WSLOT - 1)
    local_idx = local_idx.at[CAP].set(0)
    source = (src_dev * WSLOT + local_idx).astype(jnp.int32)
    return (counts.astype(jnp.int32), source)


def draw_source(key, part):
    return population(key)[1]


def draw_counts(key, part):
    return population(key)[0]


def steps_of(own_key, shape, cuts, low, top_value):
    gain, own = 1.0, jax.random.fold_in(own_key, 6)
    for dim, blocks in cuts:
        draws = jnp.exp(jax.random.uniform(jax.random.fold_in(own, dim), (blocks,), jnp.float32, low / len(cuts), top_value / len(cuts)))
        gain = gain * jnp.repeat(draws, shape[dim] // blocks).reshape([-1 if axis == dim else 1 for axis in range(len(shape))])
    return gain


def normal_values(own_key, extent, scale, limit, pieces=(), held_as=jnp.bfloat16):
    gain = steps_of(own_key, extent, pieces, -0.22, 0.18) if pieces else 1.0
    values = jax.random.normal(own_key, extent, jnp.float32) * scale * gain
    return jnp.minimum(jnp.maximum(values, -limit), limit).astype(held_as)


def setup_inputs(seed: int = 0, part: int = 0) -> dict:
    keys = jax.random.split(jax.random.key(seed), 5)
    own_keys = jax.random.split(jax.random.fold_in(keys[4], part), 5)
    return {
        "greens": normal_values(own_keys[0], (NW, NOCC, NORB), 1.0, 6.0, ((0, 16),)),
        "source": draw_source(jax.random.fold_in(jax.random.fold_in(keys[4], part), 71), part),
        "counts": draw_counts(jax.random.fold_in(jax.random.fold_in(keys[4], part), 71), part),
        "cholesky": normal_values(keys[3], (NCHOL, NOCC, NORB), (NOCC * NORB) ** -0.5, 0.0390625, ((0, 16),)),
    }


def reference(greens, source, counts, cholesky):
    slot_pos = jnp.arange(NW2) % CAP
    owner = jnp.arange(NW2) // CAP
    is_live = slot_pos < counts[owner]
    relocated = jnp.where(is_live[:, None, None], greens[source], jnp.zeros((), jnp.bfloat16)).astype(jnp.bfloat16)
    chol_flat = cholesky.reshape(NCHOL * NOCC, NORB)

    def walker_energy(walker):
        rotated = jnp.dot(chol_flat, walker.T, preferred_element_type=jnp.float32).reshape(NCHOL, NOCC, NOCC)
        return -(0.5 / NCHOL) * jnp.sum(rotated * jnp.swapaxes(rotated, 1, 2))

    exchange_energy = lax.map(walker_energy, relocated)
    force_bias = jnp.dot(relocated.reshape(NW2, NOCC * NORB), cholesky.reshape(NCHOL, NOCC * NORB).T, preferred_element_type=jnp.float32)
    return relocated, exchange_energy, force_bias
```

```python
import functools

import jax
import jax.numpy as jnp
from jax import lax
from jax.experimental import pallas as pl
from jax.experimental.pallas import tpu as pltpu
from jax.sharding import PartitionSpec as P

MESH = pl.DeviceIdType.MESH
NEAR = 3
TILE = 4
STEP = 8


def flip(index, mask):
    bit = 1
    while bit <= mask:
        if mask & bit:
            index = index + bit - 2 * bit * ((index // bit) % 2)
        bit *= 2
    return index


def kernel(
    n, nocc, chol_dev, nchol,
    source_ref, counts_ref, greens_ref, chol_ref,
    reloc_ref, energy_ref, bias_ref,
    walkers, chol, diag, message, inbox, reloc,
    local_sem, line_send, pair_send, core_send, walker_recv, mail_send, mail_recv,
):
    me = lax.axis_index("walk")
    depth = n // 4
    core = me % 2
    side = (me // 2) % 2
    z = me // 4

    def slot_of(zz, ss, cc):
        return (cc * 2 + ss) * depth + zz

    def device_of(zz, ss, cc):
        return (zz * 2 + ss) * 2 + cc

    mine = slot_of(z, side, core)
    load_own = pltpu.make_async_copy(greens_ref, walkers.at[mine], local_sem.at[0])
    load_own.start()
    load_chol = pltpu.make_async_copy(chol_ref, chol, local_sem.at[1])
    load_chol.start()

    barrier = pltpu.get_barrier_semaphore()
    for k in range(1, n):
        pl.semaphore_signal(
            barrier, inc=1, device_id={"walk": (me + k) % n}, device_id_type=MESH
        )
    diag[...] = jnp.zeros_like(diag)
    load_own.wait()
    pl.semaphore_wait(barrier, n - 1)

    def send(slot, sem, target):
        copy = pltpu.make_async_remote_copy(
            src_ref=walkers.at[slot],
            dst_ref=walkers.at[slot],
            send_sem=sem,
            recv_sem=walker_recv.at[slot],
            device_id={"walk": target},
            device_id_type=MESH,
        )
        copy.start()
        return copy

    def arrived(slot):
        pltpu.make_async_remote_copy(
            src_ref=walkers.at[slot],
            dst_ref=walkers.at[slot],
            send_sem=local_sem.at[0],
            recv_sem=walker_recv.at[slot],
            device_id={"walk": me},
            device_id_type=MESH,
        ).wait_recv()

    other = 1 - side
    sibling = device_of(z, side, 1 - core)
    partner = device_of(z, other, core)
    sent = [send(mine, pair_send.at[0], partner)]
    for k in range(1, depth):
        sent.append(send(mine, line_send.at[k], device_of(flip(z, k), side, core)))
    sent.append(send(mine, core_send.at[0], sibling))
    for k in range(1, depth):
        slot = slot_of(flip(z, k), side, core)
        arrived(slot)
        sent.append(send(slot, pair_send.at[k], partner))
        sent.append(send(slot, core_send.at[k], sibling))

    lane8 = lax.broadcasted_iota(jnp.int32, (8, 128), 1)
    row8 = lax.broadcasted_iota(jnp.int32, (8, 128), 0)
    low = lax.broadcasted_iota(jnp.int32, (nocc, 128), 1) < nocc
    on_diag = (lane8 % 8) == row8
    bands = [(lane8 % nocc) // 8 == r for r in range(nocc // 8)]
    shift = (me % 4) * chol_dev
    energy_row = pl.multiple_of((shift + chol_dev) % 128, 8)

    def compute(first):
        group = walkers[pl.ds(first, TILE)].reshape(TILE * nocc, -1)
        nt = (((1,), (1,)), ((), ()))

        def chunk(c, sums):
            rows = STEP * nocc
            part = chol[pl.ds(pl.multiple_of(c * rows, rows), rows), :]
            forward = lax.dot_general(part, group, nt, preferred_element_type=jnp.float32)
            mirror = lax.dot_general(group, part, nt, preferred_element_type=jnp.float32)
            out = []
            for wp in range(TILE // 2):
                lanes = slice(wp * 128, wp * 128 + 128)
                total = sums[wp]
                for gp in range(STEP // 2):
                    cols = slice(gp * 128, gp * 128 + 128)
                    f0 = forward[gp * 128 : gp * 128 + nocc, lanes]
                    f1 = forward[gp * 128 + nocc : gp * 128 + 128, lanes]
                    m0 = mirror[wp * 128 : wp * 128 + nocc, cols]
                    m1 = mirror[wp * 128 + nocc : wp * 128 + 128, cols]
                    turned = pltpu.roll(jnp.where(low, m1, m0), nocc, 1)
                    product = jnp.where(low, f0, f1) * jnp.where(low, m0, m1)
                    product = product + jnp.where(low, f1, f0) * turned
                    total = total + jnp.sum(product.reshape(nocc // 8, 8, 128), axis=0)
                out.append(total)
                block = jnp.zeros((8, 128), jnp.float32)
                for g in range(STEP):
                    picked = forward[g * nocc : g * nocc + 8, lanes]
                    for r in range(1, nocc // 8):
                        at = g * nocc + r * 8
                        picked = jnp.where(bands[r], forward[at : at + 8, lanes], picked)
                    line = jnp.sum(jnp.where(on_diag, picked, 0.0), axis=0, keepdims=True)
                    block = jnp.where(row8 == g, line, block)
                at = pl.multiple_of(shift + c * STEP, 8)
                diag[pl.ds(at, STEP), pl.ds(first * nocc + wp * 128, 128)] = block
            return tuple(out)

        zero = jnp.zeros((8, 128), jnp.float32)
        sums = lax.fori_loop(0, chol_dev // STEP, chunk, (zero,) * (TILE // 2))
        for wp in range(TILE // 2):
            at = pl.multiple_of(first * nocc + wp * 128, 128)
            diag[pl.ds(energy_row, 8), pl.ds(at, 128)] = sums[wp]

    def compute_group(ss, cc):
        for part in range(depth // TILE):
            compute(pl.multiple_of(slot_of(part * TILE, ss, cc), TILE))

    load_chol.wait()
    compute_group(side, core)
    for k in range(depth):
        slot = slot_of(flip(z, k), other, core)
        arrived(slot)
        sent.append(send(slot, core_send.at[depth + k], sibling))
    compute_group(other, core)
    for ss in (side, other):
        for k in range(depth):
            arrived(slot_of(flip(z, k), ss, 1 - core))
        compute_group(ss, 1 - core)

    table = jnp.sum(diag[...].T.reshape(n, nocc, 128), axis=1)
    for w in range(n):
        slot = slot_of(w // 4, (w // 2) % 2, w % 2)
        message[w + 1, :, :] = table[slot : slot + 1, :]
        if w == 0:
            message[n + 1, :, :] = table[slot : slot + 1, :]
        if w == n - 1:
            message[0, :, :] = table[slot : slot + 1, :]
    mail = []
    for k in range(1, n):
        target = (me + k) % n
        copy = pltpu.make_async_remote_copy(
            src_ref=message.at[pl.ds(target, NEAR)],
            dst_ref=inbox.at[me],
            send_sem=mail_send.at[k],
            recv_sem=mail_recv.at[me],
            device_id={"walk": target},
            device_id_type=MESH,
        )
        copy.start()
        mail.append(copy)
    inbox[pl.ds(me, 1)] = message[pl.ds(me, NEAR)][None]

    my_count = counts_ref[me]
    slots = reloc.shape[0]
    chosen = []
    for s in range(slots):
        w = jnp.clip(source_ref[s], 0, n - 1)
        slot = slot_of(w // 4, (w // 2) % 2, w % 2)
        live = s < my_count
        value = walkers[slot]
        reloc[s] = jnp.where(live, value, jnp.zeros_like(value))
        near = jnp.minimum(lax.rem(w - me + 1 + n, n), NEAR - 1)
        chosen.append((near, live))
    store = pltpu.make_async_copy(reloc, reloc_ref, local_sem.at[2])
    store.start()

    for k in range(1, n):
        origin = (me + k) % n
        pltpu.make_async_remote_copy(
            src_ref=message.at[pl.ds(0, NEAR)],
            dst_ref=inbox.at[origin],
            send_sem=local_sem.at[0],
            recv_sem=mail_recv.at[origin],
            device_id={"walk": me},
            device_id_type=MESH,
        ).wait_recv()

    lane1 = lax.broadcasted_iota(jnp.int32, (1, 128), 1)
    per = 128 // chol_dev
    for s, (near, live) in enumerate(chosen):
        energy = jnp.zeros((1, 128), jnp.float32)
        for b in range(n // per):
            row = jnp.zeros((1, 128), jnp.float32)
            for q in range(per):
                got = inbox[b * per + q, near]
                row = jnp.where(lane1 // chol_dev == q, got, row)
                rest = (lane1 + (128 - (q + 1) * chol_dev)) % 128
                energy = energy + jnp.where(rest < 8, got, 0.0)
            bias_ref[s : s + 1, b * 128 : b * 128 + 128] = jnp.where(live, row, 0.0)
        energy_ref[s] = jnp.where(live, jnp.sum(energy) * (-0.5 / nchol), 0.0)

    for copy in sent + mail:
        copy.wait_send()
    store.wait()


def body(greens, source, counts, cholesky):
    n = lax.axis_size("walk")
    chol_dev, nocc, orbitals = cholesky.shape
    slots = source.shape[0]
    nchol = chol_dev * n
    assert greens.shape[0] == 1 and nocc == 64 and chol_dev == 32
    depth = n // 4
    return pl.pallas_call(
        functools.partial(kernel, n, nocc, chol_dev, nchol),
        out_shape=(
            jax.ShapeDtypeStruct((slots, nocc, orbitals), jnp.bfloat16),
            jax.ShapeDtypeStruct((slots,), jnp.float32),
            jax.ShapeDtypeStruct((slots, nchol), jnp.float32),
        ),
        in_specs=[
            pl.BlockSpec(memory_space=pltpu.SMEM),
            pl.BlockSpec(memory_space=pltpu.SMEM),
            pl.BlockSpec(memory_space=pl.ANY),
            pl.BlockSpec(memory_space=pl.ANY),
        ],
        out_specs=(
            pl.BlockSpec(memory_space=pl.ANY),
            pl.BlockSpec(memory_space=pltpu.SMEM),
            pl.BlockSpec(memory_space=pltpu.VMEM),
        ),
        scratch_shapes=[
            pltpu.VMEM((n, nocc, orbitals), jnp.bfloat16),
            pltpu.VMEM((chol_dev * nocc, orbitals), jnp.bfloat16),
            pltpu.VMEM((128, n * nocc), jnp.float32),
            pltpu.VMEM((n + 2, 1, 128), jnp.float32),
            pltpu.VMEM((n, NEAR, 1, 128), jnp.float32),
            pltpu.VMEM((slots, nocc, orbitals), jnp.bfloat16),
            pltpu.SemaphoreType.DMA((3,)),
            pltpu.SemaphoreType.DMA((depth,)),
            pltpu.SemaphoreType.DMA((depth,)),
            pltpu.SemaphoreType.DMA((2 * depth,)),
            pltpu.SemaphoreType.DMA((n,)),
            pltpu.SemaphoreType.DMA((n,)),
            pltpu.SemaphoreType.DMA((n,)),
        ],
        compiler_params=pltpu.CompilerParams(collective_id=0, has_side_effects=True),
    )(source, counts, greens.reshape(nocc, orbitals), cholesky.reshape(chol_dev * nocc, orbitals))


def solution(mesh):
    return jax.shard_map(
        body,
        mesh=mesh,
        in_specs=(
            P(("rep", "walk"), None, None),
            P(("rep", "walk")),
            P("rep"),
            P("walk", None, None),
        ),
        out_specs=(P(("rep", "walk"), None, None), P(("rep", "walk")), P(("rep", "walk"), None)),
        check_vma=False,
    )
```

```python
import functools

import jax
import jax.numpy as jnp
from jax import lax
from jax.experimental import pallas as pl
from jax.experimental.pallas import tpu as pltpu
from jax.sharding import PartitionSpec as P

MESH = pl.DeviceIdType.MESH
NEAR = 3
TILE = 4
STEP = 8


def flip(index, mask):
    bit = 1
    while bit <= mask:
        if mask & bit:
            index = index + bit - 2 * bit * ((index // bit) % 2)
        bit *= 2
    return index


def kernel(
    n, nocc, chol_dev, nchol,
    source_ref, counts_ref, greens_ref, chol_ref,
    reloc_ref, energy_ref, bias_ref,
    walkers, chol, chol_t, group_t, diag, message, inbox, reloc,
    local_sem, line_send, pair_send, core_send, walker_recv, mail_send, mail_recv,
):
    me = lax.axis_index("walk")
    depth = n // 4
    core = me % 2
    side = (me // 2) % 2
    z = me // 4

    def slot_of(k, s, c):
        return jnp.where(k == 0, s * 2 + c, 4 + s * 2 * (depth - 1) + (k - 1) * 2 + c)

    def place(k, s, c):
        return s * 2 + c if k == 0 else 4 + s * 2 * (depth - 1) + (k - 1) * 2 + c

    def device_of(zz, ss, cc):
        return (zz * 2 + ss) * 2 + cc

    load_own = pltpu.make_async_copy(greens_ref, walkers.at[0], local_sem.at[0])
    load_own.start()
    load_chol = pltpu.make_async_copy(chol_ref, chol, local_sem.at[1])
    load_chol.start()

    barrier = pltpu.get_barrier_semaphore()
    for k in range(1, n):
        pl.semaphore_signal(
            barrier, inc=1, device_id={"walk": (me + k) % n}, device_id_type=MESH
        )
    diag[...] = jnp.zeros_like(diag)
    load_own.wait()
    pl.semaphore_wait(barrier, n - 1)

    def send(src, dst, sem, target):
        copy = pltpu.make_async_remote_copy(
            src_ref=walkers.at[src],
            dst_ref=walkers.at[dst],
            send_sem=sem,
            recv_sem=walker_recv.at[dst],
            device_id={"walk": target},
            device_id_type=MESH,
        )
        copy.start()
        sent.append(copy)

    sent = []

    def arrived(k, s, c):
        slot = place(k, s, c)
        pltpu.make_async_remote_copy(
            src_ref=walkers.at[slot],
            dst_ref=walkers.at[slot],
            send_sem=local_sem.at[0],
            recv_sem=walker_recv.at[slot],
            device_id={"walk": me},
            device_id_type=MESH,
        ).wait_recv()

    other = 1 - side
    sibling = device_of(z, side, 1 - core)
    partner = device_of(z, other, core)

    def to_partner(k):
        send(place(k, 0, 0), place(k, 1, 0), pair_send.at[k], partner)

    def to_sibling(k, s):
        send(place(k, s, 0), place(k, s, 1), core_send.at[s * depth + k], sibling)

    to_partner(0)
    for k in range(1, depth):
        send(0, place(k, 0, 0), line_send.at[k], device_of(flip(z, k), side, core))
    to_sibling(0, 0)
    load_chol.wait()

    @pl.loop(0, chol_dev // STEP)
    def _(c):
        at = pl.ds(pl.multiple_of(c * (STEP * nocc), STEP * nocc), STEP * nocc)
        chol_t[:, at] = chol[at, :].T

    lane8 = lax.broadcasted_iota(jnp.int32, (8, 128), 1)
    row8 = lax.broadcasted_iota(jnp.int32, (8, 128), 0)
    low = lax.broadcasted_iota(jnp.int32, (nocc, 128), 1) < nocc
    on_diag = (lane8 % 8) == row8
    bands = [(lane8 % nocc) // 8 == r for r in range(nocc // 8)]
    shift = (me % 4) * chol_dev
    energy_row = pl.multiple_of((shift + chol_dev) % 128, 8)

    def compute(first):
        group = walkers[first : first + TILE].reshape(TILE * nocc, -1)
        group_t[...] = group.T

        def chunk(c, sums):
            rows = STEP * nocc
            part = chol[pl.ds(pl.multiple_of(c * rows, rows), rows), :]
            part_t = chol_t[:, pl.ds(pl.multiple_of(c * rows, rows), rows)]
            forward = jnp.dot(part, group_t[...], preferred_element_type=jnp.float32)
            mirror = jnp.dot(group, part_t, preferred_element_type=jnp.float32)
            out = []
            for wp in range(TILE // 2):
                lanes = slice(wp * 128, wp * 128 + 128)
                total = sums[wp]
                for gp in range(STEP // 2):
                    cols = slice(gp * 128, gp * 128 + 128)
                    f0 = forward[gp * 128 : gp * 128 + nocc, lanes]
                    f1 = forward[gp * 128 + nocc : gp * 128 + 128, lanes]
                    m0 = mirror[wp * 128 : wp * 128 + nocc, cols]
                    m1 = mirror[wp * 128 + nocc : wp * 128 + 128, cols]
                    turned = pltpu.roll(jnp.where(low, m1, m0), nocc, 1)
                    product = jnp.where(low, f0, f1) * jnp.where(low, m0, m1)
                    product = product + jnp.where(low, f1, f0) * turned
                    total = total + jnp.sum(product.reshape(nocc // 8, 8, 128), axis=0)
                out.append(total)
                block = jnp.zeros((8, 128), jnp.float32)
                for g in range(STEP):
                    picked = forward[g * nocc : g * nocc + 8, lanes]
                    for r in range(1, nocc // 8):
                        at = g * nocc + r * 8
                        picked = jnp.where(bands[r], forward[at : at + 8, lanes], picked)
                    line = jnp.sum(jnp.where(on_diag, picked, 0.0), axis=0, keepdims=True)
                    block = jnp.where(row8 == g, line, block)
                at = pl.multiple_of(shift + c * STEP, 8)
                diag[pl.ds(at, STEP), pl.ds(first * nocc + wp * 128, 128)] = block
            return tuple(out)

        zero = jnp.zeros((8, 128), jnp.float32)
        sums = lax.fori_loop(0, chol_dev // STEP, chunk, (zero,) * (TILE // 2), unroll=True)
        for wp in range(TILE // 2):
            diag[pl.ds(energy_row, 8), pl.ds(first * nocc + wp * 128, 128)] = sums[wp]

    def from_line(k):
        arrived(k, 0, 0)
        to_partner(k)
        to_sibling(k, 0)

    def from_partner(k):
        arrived(k, 1, 0)
        to_sibling(k, 1)

    from_partner(0)
    from_line(1)
    arrived(0, 0, 1)
    arrived(0, 1, 1)
    compute(0)
    for k in range(2, depth):
        from_line(k)
    from_partner(1)
    waits = [(k, s) for s in range(2) for k in range(1, depth)]
    groups = [waits[at : at + TILE // 2] for at in range(0, len(waits), TILE // 2)]
    forwarded = 1
    for index, group in enumerate(groups):
        for k, s in group:
            if s == 1:
                while forwarded < k:
                    forwarded += 1
                    from_partner(forwarded)
            arrived(k, s, 1)
        compute((index + 1) * TILE)
        if index == 0:
            while forwarded < depth - 1:
                forwarded += 1
                from_partner(forwarded)

    table = jnp.sum(diag[...].T.reshape(n, nocc, 128), axis=1)
    for k in range(depth):
        for s in range(2):
            for c in range(2):
                at = place(k, s, c)
                w = device_of(flip(z, k), flip(side, s), flip(core, c))
                message[w + 1, :, :] = table[at : at + 1, :]
    message[0, :, :] = message[n, :, :]
    message[n + 1, :, :] = message[1, :, :]
    mail = []
    for k in range(1, n):
        target = (me + k) % n
        copy = pltpu.make_async_remote_copy(
            src_ref=message.at[pl.ds(target, NEAR)],
            dst_ref=inbox.at[me],
            send_sem=mail_send.at[k],
            recv_sem=mail_recv.at[me],
            device_id={"walk": target},
            device_id_type=MESH,
        )
        copy.start()
        mail.append(copy)
    inbox[pl.ds(me, 1)] = message[pl.ds(me, NEAR)][None]

    def slot_by(w):
        k, bit = 0, 1
        while bit < depth:
            k = k + bit * ((z // bit + w // 4 // bit) % 2)
            bit *= 2
        return slot_of(k, (side + w // 2) % 2, (core + w) % 2)

    around = [slot_by((me + n + step) % n) for step in (-1, 0, 1)]
    my_count = counts_ref[me]
    slots = reloc.shape[0]
    chosen = []
    for s in range(slots):
        near = lax.rem(jnp.clip(source_ref[s], 0, n - 1) - me + 1 + n, n)
        near = jnp.minimum(near, NEAR - 1)
        live = s < my_count
        slot = jnp.where(near == 0, around[0], jnp.where(near == 1, around[1], around[2]))
        value = walkers[slot]
        reloc[s] = jnp.where(live, value, jnp.zeros_like(value))
        chosen.append((near, live))
    store = pltpu.make_async_copy(reloc, reloc_ref, local_sem.at[2])
    store.start()

    for k in range(1, n):
        origin = (me + k) % n
        pltpu.make_async_remote_copy(
            src_ref=message.at[pl.ds(0, NEAR)],
            dst_ref=inbox.at[origin],
            send_sem=local_sem.at[0],
            recv_sem=mail_recv.at[origin],
            device_id={"walk": me},
            device_id_type=MESH,
        ).wait_recv()

    lane1 = lax.broadcasted_iota(jnp.int32, (1, 128), 1)
    per = 128 // chol_dev
    for s, (near, live) in enumerate(chosen):
        energy = jnp.zeros((1, 128), jnp.float32)
        for b in range(n // per):
            row = jnp.zeros((1, 128), jnp.float32)
            for q in range(per):
                got = inbox[b * per + q, near]
                row = jnp.where(lane1 // chol_dev == q, got, row)
                rest = (lane1 + (128 - (q + 1) * chol_dev)) % 128
                energy = energy + jnp.where(rest < 8, got, 0.0)
            bias_ref[s : s + 1, b * 128 : b * 128 + 128] = jnp.where(live, row, 0.0)
        energy_ref[s] = jnp.where(live, jnp.sum(energy) * (-0.5 / nchol), 0.0)

    for copy in sent + mail:
        copy.wait_send()
    store.wait()


def finish(reloc_ref, energy_ref, bias_ref, reloc_out, energy_out, bias_out):
    reloc_out[...] = reloc_ref[...]
    bias_out[...] = bias_ref[...]
    for s in range(energy_ref.shape[0]):
        energy_out[s] = energy_ref[s]


def body(greens, source, counts, cholesky):
    n = lax.axis_size("walk")
    chol_dev, nocc, orbitals = cholesky.shape
    slots = source.shape[0]
    nchol = chol_dev * n
    assert greens.shape[0] == 1 and nocc == 64 and chol_dev == 32
    depth = n // 4
    results = pl.pallas_call(
        functools.partial(kernel, n, nocc, chol_dev, nchol),
        out_shape=(
            jax.ShapeDtypeStruct((slots, nocc, orbitals), jnp.bfloat16),
            jax.ShapeDtypeStruct((slots,), jnp.float32),
            jax.ShapeDtypeStruct((slots, nchol), jnp.float32),
        ),
        in_specs=[
            pl.BlockSpec(memory_space=pltpu.SMEM),
            pl.BlockSpec(memory_space=pltpu.SMEM),
            pl.BlockSpec(memory_space=pl.ANY),
            pl.BlockSpec(memory_space=pl.ANY),
        ],
        out_specs=(
            pl.BlockSpec(memory_space=pl.ANY),
            pl.BlockSpec(memory_space=pltpu.SMEM),
            pl.BlockSpec(memory_space=pltpu.VMEM),
        ),
        scratch_shapes=[
            pltpu.VMEM((n, nocc, orbitals), jnp.bfloat16),
            pltpu.VMEM((chol_dev * nocc, orbitals), jnp.bfloat16),
            pltpu.VMEM((orbitals, chol_dev * nocc), jnp.bfloat16),
            pltpu.VMEM((orbitals, TILE * nocc), jnp.bfloat16),
            pltpu.VMEM((128, n * nocc), jnp.float32),
            pltpu.VMEM((n + 2, 1, 128), jnp.float32),
            pltpu.VMEM((n, NEAR, 1, 128), jnp.float32),
            pltpu.VMEM((slots, nocc, orbitals), jnp.bfloat16),
            pltpu.SemaphoreType.DMA((3,)),
            pltpu.SemaphoreType.DMA((depth,)),
            pltpu.SemaphoreType.DMA((depth,)),
            pltpu.SemaphoreType.DMA((2 * depth,)),
            pltpu.SemaphoreType.DMA((n,)),
            pltpu.SemaphoreType.DMA((n,)),
            pltpu.SemaphoreType.DMA((n,)),
        ],
        compiler_params=pltpu.CompilerParams(collective_id=0, has_side_effects=True),
    )(source, counts, greens.reshape(nocc, orbitals), cholesky.reshape(chol_dev * nocc, orbitals))
    places = [pl.BlockSpec(memory_space=m) for m in (pltpu.VMEM, pltpu.SMEM, pltpu.VMEM)]
    return pl.pallas_call(
        finish,
        out_shape=tuple(jax.ShapeDtypeStruct(x.shape, x.dtype) for x in results),
        in_specs=places,
        out_specs=tuple(places),
    )(*results)


def solution(mesh):
    return jax.shard_map(
        body,
        mesh=mesh,
        in_specs=(
            P(("rep", "walk"), None, None),
            P(("rep", "walk")),
            P("rep"),
            P("walk", None, None),
        ),
        out_specs=(P(("rep", "walk"), None, None), P(("rep", "walk")), P(("rep", "walk"), None)),
        check_vma=False,
    )
```
